32 devices in a mesh: group: 2 (over x), row: 16 (over z, y, core).
Axes of the slice: x: 2, y: 2, z: 4, core: 2. Of those that a mesh axis runs over, the one named last changes fastest.
Arguments:
- near_tiles: bfloat16 [2, 5, 1024, 1024], replicated, may hold values from -0.1875 to 0.1875
- near_order: int32 [5], replicated, may hold values from 0 to 4, each once
- receiver_basis: bfloat16 [2, 1024, 16], replicated, may hold values from -1.5 to 1.5
- source_basis: bfloat16 [2, 1024, 16], replicated, may hold values from -0.1875 to 0.1875
- coupling: float32 [2, 16, 16, 16], replicated, may hold values from -0.375 to 0.375
- initial_model: bfloat16 [2, 128, 16384], P(None, 'group', 'row'), parts along dimension 1, may hold values from -6 to 6
- observed: bfloat16 [128, 16384], P('group', 'row'), parts along dimension 0, may hold values from -18 to 18
Outputs:
- model_out: float32 [2, 128, 16384], P(None, 'group', 'row'), parts along dimension 1
- misfit: float32 [128, 16384], P('group', 'row'), parts along dimension 0
The draws below stay inside these ranges and needn't reach their ends.
There are 2 independent parts, one for each index of `group`. The reference program is written for one: setup_inputs(seed, part) draws one part's arguments, and reference() takes and returns one part's arrays. A program takes and returns all parts, laid end to end along the dimension named above; an argument that names none is the same for every part. Nothing has to cross between parts.
Inputs may be any that keep to these rules, and one draw needn't show every extreme that they name: `near_order`: a permutation of 0 to 4.
All inputs are finite; a program needn't handle non-finite values.
Results may differ from the reference program's by a relative error of at most 0.0029.
Values may be sent and summed in bfloat16 or wider, within the bound.
No kernel may reach another device: no remote copies, remote signals or barrier semaphores. Data moves between devices by JAX's collectives and lax.ppermute only.
A program may use at most 128 MiB of HBM per device.

```python
import jax
import jax.numpy as jnp
from jax import lax

PTS_DEV = 1024
PERTS = 64
LAYERS = 2
RANK = 16
RADIUS = 2
ITERS = 3
SPAN = 5
POINTS = 16384
N_ROW = 16


def shard_levels(key, dims, pieces, smallest, largest):
    level = 1.0
    for axis_at, parts in pieces:
        heights = jax.random.uniform(jax.random.fold_in(jax.random.fold_in(key, 6), axis_at), (parts,), jnp.float32, smallest / len(pieces), largest / len(pieces))
        level = level * jnp.repeat(jnp.exp(heights), dims[axis_at] // parts).reshape((-1,) + (1,) * (len(dims) - 1 - axis_at))
    return level


def normal_values(own_key, dims, scale, bound, cuts=(), kind=jnp.bfloat16):
    gain = shard_levels(own_key, dims, cuts, -0.22, 0.18) if cuts else 1.0
    values = jax.random.normal(own_key, dims, jnp.float32) * scale * gain
    return jnp.minimum(jnp.maximum(values, -bound), bound).astype(kind)


def setup_inputs(seed: int = 0, part: int = 0) -> dict:
    streams_of = jax.random.split(jax.random.key(seed), 8)
    part_keys = jax.random.split(jax.random.fold_in(streams_of[7], part), 8)
    near_tiles = normal_values(streams_of[0], (LAYERS, SPAN, PTS_DEV, PTS_DEV), PTS_DEV ** -0.5, 0.1875)
    near_order = jax.random.permutation(streams_of[1], SPAN).astype(jnp.int32)
    receiver_basis = normal_values(streams_of[2], (LAYERS, PTS_DEV, RANK), RANK ** -0.5, 1.5)
    source_basis = normal_values(streams_of[3], (LAYERS, PTS_DEV, RANK), PTS_DEV ** -0.5, 0.1875)
    coupling = normal_values(streams_of[4], (LAYERS, N_ROW, RANK, RANK), (RANK * N_ROW) ** -0.5, 0.375, (), jnp.float32)
    initial_model = normal_values(part_keys[5], (LAYERS, PERTS, POINTS), 1.0, 6.0, ((2, 16),))
    observed = normal_values(part_keys[6], (PERTS, POINTS), 3.0, 18.0, ((1, 16),))
    return {"near_tiles": near_tiles, "near_order": near_order, "receiver_basis": receiver_basis, "source_basis": source_basis, "coupling": coupling, "initial_model": initial_model, "observed": observed}


def rounded(values):
    return lax.optimization_barrier(values.astype(jnp.bfloat16)).astype(jnp.float32)


def reference(near_tiles, near_order, receiver_basis, source_basis, coupling, initial_model, observed):
    highest = lax.Precision.HIGHEST
    band_count = N_ROW
    inverse = jnp.argsort(near_order).astype(jnp.int32)
    tile_list = [near_tiles[:, inverse[offset_slot]].astype(jnp.float32) for offset_slot in range(SPAN)]
    band_offsets = jnp.arange(band_count, dtype=jnp.int32)
    far_core = coupling
    position = (band_offsets[:, None] - band_offsets[None, :]) % band_count
    chosen = far_core[:, position]
    receiver_full = receiver_basis.astype(jnp.float32)
    source_full = source_basis.astype(jnp.float32)
    model = initial_model.astype(jnp.float32).reshape(LAYERS, PERTS, band_count, PTS_DEV)
    measured = observed.astype(jnp.float32).reshape(PERTS, band_count, PTS_DEV)
    misfit = measured
    for step_index in range(ITERS):
        model_wire = rounded(model)
        predicted = jnp.zeros((PERTS, band_count, PTS_DEV), jnp.float32)
        for offset_slot in range(SPAN):
            shift_by = offset_slot - RADIUS
            moved = jnp.roll(model_wire, shift_by, axis=2)
            predicted = predicted + jnp.einsum('lpnc,lac->pna', moved, tile_list[offset_slot], precision=highest)
        summary = jnp.einsum('lpnc,lcs->lnsp', model_wire, source_full, precision=highest)
        far_field = jnp.einsum('lijrs,ljsp->lirp', chosen, summary, precision=highest)
        predicted = predicted + jnp.einsum('lar,lirp->pia', receiver_full, far_field, precision=highest)
        misfit = measured - predicted
        misfit_wire = rounded(misfit)
        gradient = jnp.zeros_like(model)
        for offset_slot in range(SPAN):
            shift_by = offset_slot - RADIUS
            moved = jnp.roll(misfit_wire, -shift_by, axis=1)
            gradient = gradient + jnp.einsum('pna,lac->lpnc', moved, tile_list[offset_slot], precision=highest)
        data_summary = jnp.einsum('lar,pia->lirp', receiver_full, misfit_wire, precision=highest)
        far_back = jnp.einsum('lijrs,lirp->ljsp', chosen, data_summary, precision=highest)
        gradient = gradient + jnp.einsum('lcs,ljsp->lpjc', source_full, far_back, precision=highest)
        model = model + 0.01 * (gradient - 10.0 * model)
    return model.reshape(LAYERS, PERTS, band_count * PTS_DEV), misfit.reshape(PERTS, band_count * PTS_DEV)
```

```python
import functools

import jax
import jax.numpy as jnp
from jax import lax
from jax.experimental import pallas as pl
from jax.experimental.pallas import tpu as pltpu
from jax.sharding import PartitionSpec as P

RADIUS = 2
ITERS = 3
SPAN = 2 * RADIUS + 1
STEP = 0.01
DAMPING = 10.0
COPIES = 3
LANES = 128
STRIP = 256
CHUNK = 512


def dot(left, right):
    return lax.dot_general(
        left, right, (((1,), (0,)), ((), ())), preferred_element_type=jnp.float32
    )


def dot_full(left, right):
    return lax.dot_general(
        left,
        right,
        (((1,), (0,)), ((), ())),
        precision=lax.Precision.HIGHEST,
        preferred_element_type=jnp.float32,
    )


def tables_kernel(
    source_ref,
    receiver_ref,
    ahead_ref,
    back_ref,
    source_wide,
    receiver_wide,
    core_ahead,
    core_back,
    receiver_rows,
    source_rows,
):
    layers, rank = source_ref.shape[:2]
    receiver_rows[...] = jnp.zeros_like(receiver_rows)
    source_rows[...] = jnp.zeros_like(source_rows)
    for l in range(layers):
        for c in range(COPIES):
            first = (l * COPIES + c) * rank
            receiver_rows[first : first + rank, :] = receiver_ref[l]
            source_rows[l, first : first + rank, :] = source_ref[l]
        source_wide[l] = jnp.concatenate([source_ref[l]] * (LANES // rank), 0).T
        receiver_wide[l] = jnp.concatenate([receiver_ref[l]] * (LANES // rank), 0).T
        before, after = l * COPIES * rank, LANES - (l + 1) * COPIES * rank
        for narrow, out in ((ahead_ref, core_ahead), (back_ref, core_back)):
            block = narrow[l]
            parts = [block] * COPIES
            if before:
                parts = [jnp.zeros((block.shape[0], before), jnp.float32)] + parts
            parts = parts + [jnp.zeros((block.shape[0], after), jnp.float32)]
            out[l] = jnp.concatenate(parts, 1)


def pack_rows(packed, bands, layers, own, cells, block_of, data_of):
    stride = layers * own
    share = cells // layers
    for l in range(layers):
        for p in range(own):
            block = block_of(l, p)
            data = data_of(p)
            for j in range(cells // LANES):
                packed[j, pl.ds(l * own + p, bands, stride=stride), :] = block[
                    :, j * LANES : (j + 1) * LANES
                ]
            for j in range(share // LANES):
                start = l * share + j * LANES
                packed[cells // LANES + j, pl.ds(l * own + p, bands, stride=stride), :] = data[
                    :, start : start + LANES
                ]


def flush(packed, out_ref):
    for j in range(packed.shape[0]):
        out_ref[:, j * LANES : (j + 1) * LANES] = packed[j].astype(out_ref.dtype)


def fetch(in_ref, packed):
    for j in range(packed.shape[0]):
        packed[j] = in_ref[:, j * LANES : (j + 1) * LANES].astype(jnp.float32)


def unpack_rows(packed, bands, layers, own, cells, store_model, store_data):
    stride = layers * own
    share = cells // layers
    for l in range(layers):
        for p in range(own):
            rows = pl.ds(l * own + p, bands, stride=stride)
            for j in range(cells // LANES):
                store_model(l, p, j * LANES, packed[j, rows, :])
            for j in range(share // LANES):
                store_data(p, l * share + j * LANES, packed[cells // LANES + j, rows, :])


def pack_kernel(model_ref, data_ref, out_ref, packed, *, bands, own):
    layers, perts, cells = model_ref.shape

    def rows_of(values, p):
        held = min(bands, perts - p * bands)
        block = values[p * bands : p * bands + held, :].astype(jnp.float32)
        if held < bands:
            block = jnp.concatenate([block, jnp.zeros((bands - held, cells), jnp.float32)], 0)
        return block

    pack_rows(
        packed,
        bands,
        layers,
        own,
        cells,
        lambda l, p: rows_of(model_ref.at[l], p),
        lambda p: rows_of(data_ref, p),
    )
    flush(packed, out_ref)


def unpack_kernel(in_ref, model_ref, data_ref, packed, *, bands, own):
    layers, perts, cells = model_ref.shape
    fetch(in_ref, packed)

    def store_model(l, p, lane, block):
        held = min(bands, perts - p * bands)
        model_ref[l, p * bands : p * bands + held, lane : lane + LANES] = block[:held]

    def store_data(p, lane, block):
        held = min(bands, perts - p * bands)
        data_ref[p * bands : p * bands + held, lane : lane + LANES] = block[:held]

    unpack_rows(packed, bands, layers, own, cells, store_model, store_data)


def rolled(values, shift, bands, own):
    shift = shift % bands
    if shift == 0:
        return values
    return jnp.concatenate(
        [pltpu.roll(values[p * bands : (p + 1) * bands], shift, 0) for p in range(own)], 0
    )


def staircase(values, sign, rank, bands, own):
    group = lax.broadcasted_iota(jnp.int32, values.shape, 1) // rank
    bit = 1
    while bit < LANES // rank:
        values = jnp.where((group & bit) != 0, rolled(values, sign * bit, bands, own), values)
        bit *= 2
    return values


def split_parts(values, rank):
    part = (lax.broadcasted_iota(jnp.int32, values.shape, 1) // rank) % COPIES
    high = values.astype(jnp.bfloat16).astype(jnp.float32)
    rest = values - high
    middle = rest.astype(jnp.bfloat16).astype(jnp.float32)
    low = rest - middle
    return jnp.where(part == 0, high, jnp.where(part == 1, middle, low)).astype(jnp.bfloat16)


def steps_kernel(
    order_ref,
    packed_in,
    tiles_hbm,
    source_wide,
    receiver_wide,
    core_ahead,
    core_back,
    receiver_rows,
    source_rows,
    packed_out,
    packed,
    model,
    measured,
    misfit,
    wire,
    tiles,
    flipped,
    sems,
    *,
    bands,
    own,
    rank,
):
    layers, span = tiles.shape[:2]
    cells = tiles.shape[3]

    def copy(j):
        part = pl.ds(j * STRIP, STRIP)
        return pltpu.make_async_copy(
            tiles_hbm.at[:, :, part, :], tiles.at[:, :, part, :], sems.at[j]
        )

    for j in range(cells // STRIP):
        copy(j).start()
    fetch(packed_in, packed)

    def store_model(l, p, lane, block):
        model[l, p * bands : (p + 1) * bands, lane : lane + LANES] = block

    def store_data(p, lane, block):
        measured[p * bands : (p + 1) * bands, lane : lane + LANES] = block

    unpack_rows(packed, bands, layers, own, cells, store_model, store_data)

    sent = wire.at[0]
    slots = []
    for offset in range(span):
        slot = jnp.int32(0)
        for k in range(1, span):
            slot = slot + jnp.where(order_ref[k] == offset, k, 0)
        slots.append(slot)
    groups = bands // (LANES // rank)

    def far(wide, cores, sign):
        total = jnp.zeros((bands * own, LANES), jnp.float32)
        for l in range(layers):
            stair = staircase(wide[l], sign, rank, bands, own)

            def add(g, carry, l=l):
                moved, total = carry
                start = pl.multiple_of(g * LANES, LANES)
                total = total + dot_full(moved, cores[l, pl.ds(start, LANES), :])
                return rolled(moved, sign * (LANES // rank), bands, own), total

            total = lax.fori_loop(0, groups, add, (stair, total), unroll=groups <= 2)[1]
        return split_parts(total, rank)

    def step(first):
        wide = []
        for l in range(layers):
            value = model[l]
            for offset in range(span):
                wire[l, slots[offset]] = rolled(value, offset - RADIUS, bands, own).astype(
                    jnp.bfloat16
                )
            wide.append(dot(value.astype(jnp.bfloat16), source_wide[l]))
        field = far(wide, core_ahead, 1)
        for j in range(cells // STRIP):
            part = slice(j * STRIP, (j + 1) * STRIP)
            if first:
                copy(j).wait()
            predicted = dot(field, receiver_rows[:, part])
            for l in range(layers):
                for k in range(span):
                    if first:
                        block = tiles[l, k, part, :].T
                        flipped[l, k, :, part] = block
                    else:
                        block = flipped[l, k, :, part]
                    predicted = predicted + dot(wire[l, k], block)
            misfit[:, part] = measured[:, part] - predicted
        residual = misfit[...]
        for offset in range(span):
            sent[slots[offset]] = rolled(residual, RADIUS - offset, bands, own).astype(
                jnp.bfloat16
            )
        rounded = residual.astype(jnp.bfloat16)
        back = far([dot(rounded, receiver_wide[l]) for l in range(layers)], core_back, -1)
        for l in range(layers):
            for j in range(cells // CHUNK):
                part = slice(j * CHUNK, (j + 1) * CHUNK)
                gradient = dot(back, source_rows[l, :, part])
                for k in range(span):
                    gradient = gradient + dot(sent[k], tiles[l, k, :, part])
                value = model[l, :, part]
                model[l, :, part] = value + STEP * (gradient - DAMPING * value)

    step(True)
    lax.fori_loop(1, ITERS, lambda index, carry: (step(False), carry)[1], 0)
    pack_rows(
        packed,
        bands,
        layers,
        own,
        cells,
        lambda l, p: model[l, p * bands : (p + 1) * bands, :],
        lambda p: misfit[p * bands : (p + 1) * bands, :],
    )
    flush(packed, packed_out)


def whole_array():
    return pl.BlockSpec(memory_space=pltpu.VMEM)


def on_device(
    near_tiles, near_order, receiver_basis, source_basis, coupling, initial_model, observed, *, bands
):
    layers, perts, cells = initial_model.shape
    rank = coupling.shape[-1]
    own = -(-perts // bands)
    held = layers * own
    rows = bands * held
    width = cells + cells // layers
    cols = bands * own
    bf16, f32 = jnp.bfloat16, jnp.float32

    packed = pl.pallas_call(
        functools.partial(pack_kernel, bands=bands, own=own),
        out_shape=jax.ShapeDtypeStruct((rows, width), bf16),
        in_specs=[whole_array()] * 2,
        out_specs=whole_array(),
        scratch_shapes=[pltpu.VMEM((width // LANES, rows, LANES), f32)],
        name="pack",
    )(initial_model, observed)
    received = lax.all_to_all(packed.reshape(bands, held, width), "row", 0, 0, tiled=True)

    span = near_tiles.shape[1]
    tables = pl.pallas_call(
        tables_kernel,
        out_shape=[
            jax.ShapeDtypeStruct((layers, cells, LANES), bf16),
            jax.ShapeDtypeStruct((layers, cells, LANES), bf16),
            jax.ShapeDtypeStruct((layers, bands * rank, LANES), f32),
            jax.ShapeDtypeStruct((layers, bands * rank, LANES), f32),
            jax.ShapeDtypeStruct((LANES, cells), bf16),
            jax.ShapeDtypeStruct((layers, LANES, cells), bf16),
        ],
        in_specs=[whole_array()] * 4,
        out_specs=[whole_array()] * 6,
        name="tables",
    )(
        source_basis.transpose(0, 2, 1),
        receiver_basis.transpose(0, 2, 1),
        coupling.transpose(0, 1, 3, 2).reshape(layers, bands * rank, rank),
        coupling.reshape(layers, bands * rank, rank),
    )

    result = pl.pallas_call(
        functools.partial(steps_kernel, bands=bands, own=own, rank=rank),
        out_shape=jax.ShapeDtypeStruct((rows, width), bf16),
        in_specs=[
            pl.BlockSpec(memory_space=pltpu.SMEM),
            whole_array(),
            pl.BlockSpec(memory_space=pl.ANY),
        ]
        + [whole_array()] * 6,
        out_specs=whole_array(),
        scratch_shapes=[
            pltpu.VMEM((width // LANES, rows, LANES), f32),
            pltpu.VMEM((layers, cols, cells), f32),
            pltpu.VMEM((cols, cells), f32),
            pltpu.VMEM((cols, cells), f32),
            pltpu.VMEM((layers, span, cols, cells), bf16),
            pltpu.VMEM(near_tiles.shape, bf16),
            pltpu.VMEM(near_tiles.shape, bf16),
            pltpu.SemaphoreType.DMA((cells // STRIP,)),
        ],
        compiler_params=pltpu.CompilerParams(vmem_limit_bytes=60 << 20),
        name="steps",
    )(
        near_order,
        received.reshape(rows, width),
        near_tiles,
        *tables,
    )
    returned = lax.all_to_all(result.reshape(bands, held, width), "row", 0, 0, tiled=True)
    return pl.pallas_call(
        functools.partial(unpack_kernel, bands=bands, own=own),
        out_shape=(
            jax.ShapeDtypeStruct((layers, perts, cells), f32),
            jax.ShapeDtypeStruct((perts, cells), f32),
        ),
        in_specs=[whole_array()],
        out_specs=(whole_array(), whole_array()),
        scratch_shapes=[pltpu.VMEM((width // LANES, rows, LANES), f32)],
        name="unpack",
    )(returned.reshape(rows, width))


def solution(mesh):
    placed = (P(), P(), P(), P(), P(), P(None, "group", "row"), P("group", "row"))
    return jax.shard_map(
        functools.partial(on_device, bands=mesh.shape["row"]),
        mesh=mesh,
        in_specs=placed,
        out_specs=(P(None, "group", "row"), P("group", "row")),
        check_vma=False,
    )
```

```python
import functools

import jax
import jax.numpy as jnp
from jax import lax
from jax.experimental import pallas as pl
from jax.experimental.pallas import tpu as pltpu
from jax.sharding import PartitionSpec as P

RADIUS = 2
ITERS = 3
SPAN = 2 * RADIUS + 1
STEP = 0.01
DAMPING = 10.0
COPIES = 3
LANES = 128
STRIP = 256
CHUNK = 512
SMALL = 8 << 20


def dot(left, right):
    return lax.dot_general(
        left, right, (((1,), (0,)), ((), ())), preferred_element_type=jnp.float32
    )


def dot_full(left, right):
    return lax.dot_general(
        left,
        right,
        (((1,), (0,)), ((), ())),
        precision=lax.Precision.HIGHEST,
        preferred_element_type=jnp.float32,
    )


def tables_kernel(
    source_ref,
    receiver_ref,
    ahead_ref,
    back_ref,
    source_wide,
    receiver_wide,
    core_ahead,
    core_back,
    receiver_rows,
    source_rows,
):
    layers, rank = source_ref.shape[:2]
    receiver_rows[...] = jnp.zeros_like(receiver_rows)
    source_rows[...] = jnp.zeros_like(source_rows)
    for l in range(layers):
        for c in range(COPIES):
            first = (l * COPIES + c) * rank
            receiver_rows[first : first + rank, :] = receiver_ref[l]
            source_rows[l, first : first + rank, :] = source_ref[l]
        source_wide[l] = jnp.concatenate([source_ref[l]] * (LANES // rank), 0).T
        receiver_wide[l] = jnp.concatenate([receiver_ref[l]] * (LANES // rank), 0).T
        before, after = l * COPIES * rank, LANES - (l + 1) * COPIES * rank
        for narrow, out in ((ahead_ref, core_ahead), (back_ref, core_back)):
            block = narrow[l]
            parts = [block] * COPIES
            if before:
                parts = [jnp.zeros((block.shape[0], before), jnp.float32)] + parts
            parts = parts + [jnp.zeros((block.shape[0], after), jnp.float32)]
            out[l] = jnp.concatenate(parts, 1)


def exchanged(first, second, own):
    shape = first.shape
    first = first.reshape(-1, 2 * own, shape[-1])
    second = second.reshape(-1, 2 * own, shape[-1])
    low = lax.broadcasted_iota(jnp.int32, first.shape, 1) < own
    even = jnp.where(low, first, pltpu.roll(second, own, 1))
    odd = jnp.where(low, pltpu.roll(first, own, 1), second)
    return even, odd


def merged(first, second, own):
    even, odd = exchanged(first, second, own)
    return jnp.stack([even, odd], 1).reshape(-1, first.shape[-1])


def parted(values, own):
    pairs = values.reshape(-1, 2, 2 * own, values.shape[-1])
    low = lax.broadcasted_iota(jnp.int32, pairs[:, 0].shape, 1) < own
    even, odd = pairs[:, 0], pairs[:, 1]
    first = jnp.where(low, even, pltpu.roll(odd, own, 1))
    second = jnp.where(low, pltpu.roll(even, own, 1), odd)
    return first.reshape(-1, values.shape[-1]), second.reshape(-1, values.shape[-1])


def pack_kernel(model_ref, data_ref, out_ref, *, own):
    cells = model_ref.shape[-1]
    half = cells // 2
    f32 = jnp.float32
    out_ref[:, :cells] = merged(
        model_ref[0].astype(f32), model_ref[1].astype(f32), own
    ).astype(out_ref.dtype)
    out_ref[:, cells:] = merged(
        data_ref[:, :half].astype(f32), data_ref[:, half:].astype(f32), own
    ).astype(out_ref.dtype)


def unpack_kernel(in_ref, model_ref, data_ref, *, own):
    cells = model_ref.shape[-1]
    half = cells // 2
    model_ref[0], model_ref[1] = parted(in_ref[:, :cells].astype(jnp.float32), own)
    data_ref[:, :half], data_ref[:, half:] = parted(
        in_ref[:, cells:].astype(jnp.float32), own
    )


def rolled(values, shift, own):
    shift = (shift * own) % values.shape[0]
    return pltpu.roll(values, shift, 0) if shift else values


def staircase(values, sign, rank, own):
    group = lax.broadcasted_iota(jnp.int32, values.shape, 1) // rank
    bit = 1
    while bit < LANES // rank:
        values = jnp.where((group & bit) != 0, rolled(values, sign * bit, own), values)
        bit *= 2
    return values


def split_parts(values, rank):
    part = (lax.broadcasted_iota(jnp.int32, values.shape, 1) // rank) % COPIES
    high = values.astype(jnp.bfloat16).astype(jnp.float32)
    rest = values - high
    middle = rest.astype(jnp.bfloat16).astype(jnp.float32)
    low = rest - middle
    return jnp.where(part == 0, high, jnp.where(part == 1, middle, low)).astype(jnp.bfloat16)


def steps_kernel(
    order_ref,
    packed_in,
    tiles_hbm,
    source_wide,
    receiver_wide,
    core_ahead,
    core_back,
    receiver_rows,
    source_rows,
    packed_out,
    model,
    measured,
    misfit,
    wire,
    tiles,
    flipped,
    sems,
    *,
    bands,
    own,
    rank,
    paired,
):
    layers, span = tiles.shape[:2]
    cells = tiles.shape[3]
    share = cells // layers
    cols = bands * own

    def copy(j):
        part = pl.ds(j * STRIP, STRIP)
        return pltpu.make_async_copy(
            tiles_hbm.at[:, :, part, :], tiles.at[:, :, part, :], sems.at[j]
        )

    for j in range(cells // STRIP):
        copy(j).start()
    if paired:
        model[0], model[1] = parted(packed_in[:, :cells].astype(jnp.float32), own)
        measured[:, :share], measured[:, share:] = parted(
            packed_in[:, cells:].astype(jnp.float32), own
        )
    else:
        for l in range(layers):
            rows = slice(l * cols, (l + 1) * cols)
            model[l] = packed_in[rows, :cells].astype(jnp.float32)
            measured[:, l * share : (l + 1) * share] = packed_in[rows, cells:].astype(jnp.float32)

    sent = wire.at[0]
    slots = []
    for offset in range(span):
        slot = jnp.int32(0)
        for k in range(1, span):
            slot = slot + jnp.where(order_ref[k] == offset, k, 0)
        slots.append(slot)
    groups = bands // (LANES // rank)

    def far(wide, cores, sign):
        total = jnp.zeros((cols, LANES), jnp.float32)
        for l in range(layers):
            stair = staircase(wide[l], sign, rank, own)

            def add(g, carry, l=l):
                moved, total = carry
                start = pl.multiple_of(g * LANES, LANES)
                total = total + dot_full(moved, cores[l, pl.ds(start, LANES), :])
                return rolled(moved, sign * (LANES // rank), own), total

            total = lax.fori_loop(0, groups, add, (stair, total), unroll=groups <= 2)[1]
        return split_parts(total, rank)

    def step(first):
        wide = []
        for l in range(layers):
            value = model[l]
            for offset in range(span):
                wire[l, slots[offset]] = rolled(value, offset - RADIUS, own).astype(jnp.bfloat16)
            wide.append(dot(value.astype(jnp.bfloat16), source_wide[l]))
        strips = cells // STRIP
        for j in range(strips):
            part = slice(j * STRIP, (j + 1) * STRIP)
            if first:
                copy(j).wait()
            predicted = None
            for l in range(layers):
                for k in range(span):
                    if first:
                        block = tiles[l, k, part, :].T
                        flipped[l, k, :, part] = block
                    else:
                        block = flipped[l, k, :, part]
                    term = dot(wire[l, k], block)
                    predicted = term if predicted is None else predicted + term
            misfit[:, part] = measured[:, part] - predicted
            if j == 0:
                field = far(wide, core_ahead, 1)
        residual = misfit[...] - dot(field, receiver_rows[...])
        misfit[...] = residual
        for offset in range(span):
            sent[slots[offset]] = rolled(residual, RADIUS - offset, own).astype(jnp.bfloat16)
        rounded = residual.astype(jnp.bfloat16)
        wide = [dot(rounded, receiver_wide[l]) for l in range(layers)]
        for l in range(layers):
            for j in range(cells // CHUNK):
                part = slice(j * CHUNK, (j + 1) * CHUNK)
                gradient = None
                for k in range(span):
                    term = dot(sent[k], tiles[l, k, :, part])
                    gradient = term if gradient is None else gradient + term
                if l + j == 0:
                    back = far(wide, core_back, -1)
                gradient = gradient + dot(back, source_rows[l, :, part])
                value = model[l, :, part]
                model[l, :, part] = value + STEP * (gradient - DAMPING * value)

    step(True)
    lax.fori_loop(1, ITERS, lambda index, carry: (step(False), carry)[1], 0)
    if paired:
        packed_out[:, :cells] = merged(model[0], model[1], own).astype(packed_out.dtype)
        packed_out[:, cells:] = merged(misfit[:, :share], misfit[:, share:], own).astype(
            packed_out.dtype
        )
    else:
        for l in range(layers):
            rows = slice(l * cols, (l + 1) * cols)
            packed_out[rows, :cells] = model[l].astype(packed_out.dtype)
            packed_out[rows, cells:] = misfit[:, l * share : (l + 1) * share].astype(
                packed_out.dtype
            )


def whole_array():
    return pl.BlockSpec(memory_space=pltpu.VMEM)


def on_device(
    near_tiles, near_order, receiver_basis, source_basis, coupling, initial_model, observed, *, bands
):
    layers, perts, cells = initial_model.shape
    rank = coupling.shape[-1]
    own = -(-perts // bands)
    held = layers * own
    rows = bands * held
    width = cells + cells // layers
    cols = bands * own
    bf16, f32 = jnp.bfloat16, jnp.float32

    paired = layers == 2 and layers * own == 8 and perts == cols
    small = pltpu.CompilerParams(vmem_limit_bytes=SMALL)
    if paired:
        packed = pl.pallas_call(
            functools.partial(pack_kernel, own=own),
            out_shape=jax.ShapeDtypeStruct((rows, width), bf16),
            in_specs=[whole_array()] * 2,
            out_specs=whole_array(),
            compiler_params=small,
            name="pack",
        )(initial_model, observed)
    else:
        padding = cols - perts
        parts = jnp.pad(initial_model, ((0, 0), (0, padding), (0, 0)))
        parts = parts.reshape(layers, bands, own, cells).transpose(1, 0, 2, 3)
        data = jnp.pad(observed, ((0, padding), (0, 0)))
        data = data.reshape(bands, own, layers, cells // layers).transpose(0, 2, 1, 3)
        packed = jnp.concatenate([parts, data], -1)
    received = lax.all_to_all(packed.reshape(bands, held, width), "row", 0, 0, tiled=True)
    if not paired:
        received = received.reshape(bands, layers, own, width).transpose(1, 0, 2, 3)

    span = near_tiles.shape[1]
    tables = pl.pallas_call(
        tables_kernel,
        out_shape=[
            jax.ShapeDtypeStruct((layers, cells, LANES), bf16),
            jax.ShapeDtypeStruct((layers, cells, LANES), bf16),
            jax.ShapeDtypeStruct((layers, bands * rank, LANES), f32),
            jax.ShapeDtypeStruct((layers, bands * rank, LANES), f32),
            jax.ShapeDtypeStruct((LANES, cells), bf16),
            jax.ShapeDtypeStruct((layers, LANES, cells), bf16),
        ],
        in_specs=[whole_array()] * 4,
        out_specs=[whole_array()] * 6,
        compiler_params=small,
        name="tables",
    )(
        source_basis.transpose(0, 2, 1),
        receiver_basis.transpose(0, 2, 1),
        coupling.transpose(0, 1, 3, 2).reshape(layers, bands * rank, rank),
        coupling.reshape(layers, bands * rank, rank),
    )

    limit = 4 * near_tiles.size + 40 * 4 * cols * cells
    result = pl.pallas_call(
        functools.partial(steps_kernel, bands=bands, own=own, rank=rank, paired=paired),
        out_shape=jax.ShapeDtypeStruct((rows, width), bf16),
        in_specs=[
            pl.BlockSpec(memory_space=pltpu.SMEM),
            whole_array(),
            pl.BlockSpec(memory_space=pl.ANY),
        ]
        + [whole_array()] * 6,
        out_specs=whole_array(),
        scratch_shapes=[
            pltpu.VMEM((layers, cols, cells), f32),
            pltpu.VMEM((cols, cells), f32),
            pltpu.VMEM((cols, cells), f32),
            pltpu.VMEM((layers, span, cols, cells), bf16),
            pltpu.VMEM(near_tiles.shape, bf16),
            pltpu.VMEM(near_tiles.shape, bf16),
            pltpu.SemaphoreType.DMA((cells // STRIP,)),
        ],
        compiler_params=pltpu.CompilerParams(vmem_limit_bytes=limit),
        name="steps",
    )(
        near_order,
        received.reshape(rows, width),
        near_tiles,
        *tables,
    )
    if not paired:
        result = result.reshape(layers, bands, own, width).transpose(1, 0, 2, 3)
    returned = lax.all_to_all(result.reshape(bands, held, width), "row", 0, 0, tiled=True)
    if paired:
        return pl.pallas_call(
            functools.partial(unpack_kernel, own=own),
            out_shape=(
                jax.ShapeDtypeStruct((layers, perts, cells), f32),
                jax.ShapeDtypeStruct((perts, cells), f32),
            ),
            in_specs=[whole_array()],
            out_specs=(whole_array(), whole_array()),
            compiler_params=small,
            name="unpack",
        )(returned.reshape(rows, width))
    returned = returned.reshape(bands, layers, own, width).astype(f32)
    model = returned[..., :cells].transpose(1, 0, 2, 3).reshape(layers, cols, cells)
    misfit = returned[..., cells:].transpose(0, 2, 1, 3).reshape(cols, cells)
    return model[:, :perts], misfit[:perts]


def solution(mesh):
    placed = (P(), P(), P(), P(), P(), P(None, "group", "row"), P("group", "row"))
    return jax.shard_map(
        functools.partial(on_device, bands=mesh.shape["row"]),
        mesh=mesh,
        in_specs=placed,
        out_specs=(P(None, "group", "row"), P("group", "row")),
        check_vma=False,
    )
```

```python
import functools

import jax
import jax.numpy as jnp
from jax import lax
from jax.experimental import pallas as pl
from jax.experimental.pallas import tpu as pltpu
from jax.sharding import PartitionSpec as P

RADIUS = 2
ITERS = 3
SPAN = 2 * RADIUS + 1
STEP = 0.01
DAMPING = 10.0
COPIES = 3
LANES = 128
STRIP = 256
EARLY = 2
CHUNK = 512
SMALL = 8 << 20


def dot(left, right):
    return lax.dot_general(
        left, right, (((1,), (0,)), ((), ())), preferred_element_type=jnp.float32
    )


def dot_full(left, right):
    return lax.dot_general(
        left,
        right,
        (((1,), (0,)), ((), ())),
        precision=lax.Precision.HIGHEST,
        preferred_element_type=jnp.float32,
    )


def tables(
    source_ref,
    receiver_ref,
    coupling_ref,
    source_wide,
    receiver_wide,
    core_ahead,
    core_back,
    receiver_rows,
    source_rows,
):
    layers, rank = source_ref.shape[:2]
    receiver_rows[...] = jnp.zeros_like(receiver_rows)
    source_rows[...] = jnp.zeros_like(source_rows)
    for l in range(layers):
        for c in range(COPIES):
            first = (l * COPIES + c) * rank
            receiver_rows[first : first + rank, :] = receiver_ref[l]
            source_rows[l, first : first + rank, :] = source_ref[l]
        source_wide[l] = jnp.concatenate([source_ref[l]] * (LANES // rank), 0).T
        receiver_wide[l] = jnp.concatenate([receiver_ref[l]] * (LANES // rank), 0).T
        before, after = l * COPIES * rank, LANES - (l + 1) * COPIES * rank
        back = coupling_ref[l]
        count = back.shape[0]
        turned = jnp.concatenate([back, jnp.zeros((count, LANES - rank), jnp.float32)], 1).T
        ahead = jnp.concatenate(
            [turned[:rank, first : first + rank] for first in range(0, count, rank)], 0
        )
        for block, out in ((ahead, core_ahead), (back, core_back)):
            parts = [block] * COPIES
            if before:
                parts = [jnp.zeros((count, before), jnp.float32)] + parts
            parts = parts + [jnp.zeros((count, after), jnp.float32)]
            out[l] = jnp.concatenate(parts, 1)


def merged(first, second, own):
    lanes = first.shape[-1]
    first = first.reshape(-1, 2 * own, lanes)
    second = second.reshape(-1, 2 * own, lanes)
    low = lax.broadcasted_iota(jnp.int32, first.shape, 1) < own
    even = jnp.where(low, first, pltpu.roll(second, own, 1))
    odd = jnp.where(low, pltpu.roll(first, own, 1), second)
    return jnp.stack([even, odd], 1).reshape(-1, lanes)


def parted(values, own):
    pairs = values.reshape(-1, 2, 2 * own, values.shape[-1])
    low = lax.broadcasted_iota(jnp.int32, pairs[:, 0].shape, 1) < own
    even, odd = pairs[:, 0], pairs[:, 1]
    first = jnp.where(low, even, pltpu.roll(odd, own, 1))
    second = jnp.where(low, pltpu.roll(even, own, 1), odd)
    return first.reshape(-1, values.shape[-1]), second.reshape(-1, values.shape[-1])


def pack_kernel(model_hbm, data_hbm, out_ref, model_ref, data_ref, sems, *, own):
    cells = model_ref.shape[-1]
    half = cells // 2
    f32 = jnp.float32
    model_copy = pltpu.make_async_copy(model_hbm, model_ref, sems.at[0])
    data_copy = pltpu.make_async_copy(data_hbm, data_ref, sems.at[1])
    model_copy.start()
    data_copy.start()
    model_copy.wait()
    out_ref[:, :cells] = merged(
        model_ref[0].astype(f32), model_ref[1].astype(f32), own
    ).astype(out_ref.dtype)
    data_copy.wait()
    out_ref[:, cells:] = merged(
        data_ref[:, :half].astype(f32), data_ref[:, half:].astype(f32), own
    ).astype(out_ref.dtype)


def ready_kernel(
    source_hbm,
    receiver_hbm,
    coupling_hbm,
    tiles_hbm,
    source_wide,
    receiver_wide,
    core_ahead,
    core_back,
    receiver_rows,
    source_rows,
    flipped_hbm,
    source_ref,
    receiver_ref,
    coupling_ref,
    natural,
    flipped,
    small_sems,
    in_sems,
    out_sems,
):
    layers = tiles_hbm.shape[0]
    small = [
        pltpu.make_async_copy(source, target, small_sems.at[n])
        for n, (source, target) in enumerate(
            (
                (source_hbm, source_ref),
                (receiver_hbm, receiver_ref),
                (coupling_hbm, coupling_ref),
            )
        )
    ]
    pairs = [(l, k) for l in range(layers) for k in range(EARLY)]
    arrive = [
        pltpu.make_async_copy(tiles_hbm.at[l, k], natural.at[l, k], in_sems.at[n])
        for n, (l, k) in enumerate(pairs)
    ]
    leave = [
        pltpu.make_async_copy(flipped.at[l, k], flipped_hbm.at[l, k], out_sems.at[n])
        for n, (l, k) in enumerate(pairs)
    ]
    for copy in small + arrive:
        copy.start()
    for n, (l, k) in enumerate(pairs):
        arrive[n].wait()
        for first in range(0, natural.shape[2], STRIP):
            part = slice(first, first + STRIP)
            flipped[l, k, :, part] = natural[l, k, part, :].T
        leave[n].start()
    for copy in small:
        copy.wait()
    tables(
        source_ref,
        receiver_ref,
        coupling_ref,
        source_wide,
        receiver_wide,
        core_ahead,
        core_back,
        receiver_rows,
        source_rows,
    )
    for copy in leave:
        copy.wait()


def unpack_kernel(in_ref, model_ref, data_ref, *, own):
    cells = model_ref.shape[-1]
    half = cells // 2
    model_ref[0], model_ref[1] = parted(in_ref[:, :cells].astype(jnp.float32), own)
    data_ref[:, :half], data_ref[:, half:] = parted(
        in_ref[:, cells:].astype(jnp.float32), own
    )


def rolled(values, shift, own):
    shift = (shift * own) % values.shape[0]
    return pltpu.roll(values, shift, 0) if shift else values


def staircase(values, sign, rank, own):
    group = lax.broadcasted_iota(jnp.int32, values.shape, 1) // rank
    bit = 1
    while bit < LANES // rank:
        values = jnp.where((group & bit) != 0, rolled(values, sign * bit, own), values)
        bit *= 2
    return values


def split_parts(values, rank):
    part = (lax.broadcasted_iota(jnp.int32, values.shape, 1) // rank) % COPIES
    high = values.astype(jnp.bfloat16).astype(jnp.float32)
    rest = values - high
    middle = rest.astype(jnp.bfloat16).astype(jnp.float32)
    low = rest - middle
    return jnp.where(part == 0, high, jnp.where(part == 1, middle, low)).astype(jnp.bfloat16)


def steps_kernel(
    order_hbm,
    packed_in,
    tiles_hbm,
    flipped_hbm,
    source_wide,
    receiver_wide,
    core_ahead,
    core_back,
    receiver_rows,
    source_rows,
    packed_out,
    model,
    measured,
    misfit,
    wire,
    sent,
    tiles,
    flipped,
    order_ref,
    order_sem,
    strip_sems,
    late_sems,
    *,
    bands,
    own,
    rank,
    paired,
):
    layers, span = tiles.shape[:2]
    cells = tiles.shape[3]
    share = cells // layers
    cols = bands * own

    strips = cells // STRIP

    def piece(j, l, k):
        part = pl.ds(j * STRIP, STRIP)
        sem = strip_sems.at[j, l, k]
        if k < EARLY:
            return pltpu.make_async_copy(
                flipped_hbm.at[l, k, :, part], flipped.at[l, k, :, part], sem
            )
        return pltpu.make_async_copy(tiles_hbm.at[l, k, part, :], tiles.at[l, k, part, :], sem)

    def late(l, k):
        return pltpu.make_async_copy(tiles_hbm.at[l, k], tiles.at[l, k], late_sems.at[l, k])

    order = pltpu.make_async_copy(order_hbm, order_ref, order_sem)
    order.start()
    for j in range(strips):
        for l in range(layers):
            for k in range(span):
                piece(j, l, k).start()
    for l in range(layers):
        for k in range(EARLY):
            late(l, k).start()
    if paired:
        model[0], model[1] = parted(packed_in[:, :cells].astype(jnp.float32), own)
        measured[:, :share], measured[:, share:] = parted(
            packed_in[:, cells:].astype(jnp.float32), own
        )
    else:
        for l in range(layers):
            rows = slice(l * cols, (l + 1) * cols)
            model[l] = packed_in[rows, :cells].astype(jnp.float32)
            measured[:, l * share : (l + 1) * share] = packed_in[rows, cells:].astype(jnp.float32)

    order.wait()
    slots = []
    for offset in range(span):
        slot = jnp.int32(0)
        for k in range(1, span):
            slot = slot + jnp.where(order_ref[k] == offset, k, 0)
        slots.append(slot)
    groups = bands // (LANES // rank)

    def far(wide, cores, sign):
        total = jnp.zeros((cols, LANES), jnp.float32)
        for l in range(layers):
            stair = staircase(wide[l], sign, rank, own)

            def add(g, carry, l=l):
                moved, total = carry
                start = pl.multiple_of(g * LANES, LANES)
                total = total + dot_full(moved, cores[l, pl.ds(start, LANES), :])
                return rolled(moved, sign * (LANES // rank), own), total

            total = lax.fori_loop(0, groups, add, (stair, total), unroll=groups <= 2)[1]
        return split_parts(total, rank)

    def send(l):
        value = model[l]
        for offset in range(span):
            wire[l, slots[offset]] = rolled(value, offset - RADIUS, own).astype(jnp.bfloat16)

    def step(first):
        wide = [dot(model[l].astype(jnp.bfloat16), source_wide[l]) for l in range(layers)]
        for j in range(strips):
            part = slice(j * STRIP, (j + 1) * STRIP)
            predicted = None
            for l in range(layers):
                for k in range(span):
                    if first:
                        piece(j, l, k).wait()
                    if first and k >= EARLY:
                        block = tiles[l, k, part, :].T
                        flipped[l, k, :, part] = block
                    else:
                        block = flipped[l, k, :, part]
                    term = dot(wire[l, k], block)
                    predicted = term if predicted is None else predicted + term
            misfit[:, part] = measured[:, part] - predicted
            if j == 0:
                field = far(wide, core_ahead, 1)
        residual = misfit[...] - dot(field, receiver_rows[...])
        misfit[...] = residual
        for offset in range(span):
            sent[slots[offset]] = rolled(residual, RADIUS - offset, own).astype(jnp.bfloat16)
        rounded = residual.astype(jnp.bfloat16)
        wide = [dot(rounded, receiver_wide[l]) for l in range(layers)]
        for l in range(layers):
            if first:
                for k in range(EARLY):
                    late(l, k).wait()
            for j in range(cells // CHUNK):
                part = slice(j * CHUNK, (j + 1) * CHUNK)
                gradient = None
                for k in range(span):
                    term = dot(sent[k], tiles[l, k, :, part])
                    gradient = term if gradient is None else gradient + term
                if l + j == 0:
                    back = far(wide, core_back, -1)
                gradient = gradient + dot(back, source_rows[l, :, part])
                value = model[l, :, part]
                model[l, :, part] = value + STEP * (gradient - DAMPING * value)
            send(l)

    for l in range(layers):
        send(l)
    step(True)
    lax.fori_loop(1, ITERS, lambda index, carry: (step(False), carry)[1], 0)
    if paired:
        packed_out[:, :cells] = merged(model[0], model[1], own).astype(packed_out.dtype)
        packed_out[:, cells:] = merged(misfit[:, :share], misfit[:, share:], own).astype(
            packed_out.dtype
        )
    else:
        for l in range(layers):
            rows = slice(l * cols, (l + 1) * cols)
            packed_out[rows, :cells] = model[l].astype(packed_out.dtype)
            packed_out[rows, cells:] = misfit[:, l * share : (l + 1) * share].astype(
                packed_out.dtype
            )


def whole_array():
    return pl.BlockSpec(memory_space=pltpu.VMEM)


def in_place():
    return pl.BlockSpec(memory_space=pltpu.HBM)


def stay(value):
    return pltpu.with_memory_space_constraint(value, pltpu.HBM)


def on_device(
    near_tiles, near_order, receiver_basis, source_basis, coupling, initial_model, observed, *, bands
):
    layers, perts, cells = initial_model.shape
    rank = coupling.shape[-1]
    own = -(-perts // bands)
    held = layers * own
    rows = bands * held
    width = cells + cells // layers
    cols = bands * own
    bf16, f32 = jnp.bfloat16, jnp.float32

    paired = layers == 2 and layers * own == 8 and perts == cols
    small = pltpu.CompilerParams(vmem_limit_bytes=SMALL)
    span = near_tiles.shape[1]
    if paired:
        packed = pl.pallas_call(
            functools.partial(pack_kernel, own=own),
            out_shape=jax.ShapeDtypeStruct((rows, width), bf16),
            in_specs=[in_place()] * 2,
            out_specs=whole_array(),
            scratch_shapes=[
                pltpu.VMEM(initial_model.shape, bf16),
                pltpu.VMEM(observed.shape, bf16),
                pltpu.SemaphoreType.DMA((2,)),
            ],
            compiler_params=small,
            name="pack",
        )(stay(initial_model), stay(observed))
    else:
        padding = cols - perts
        parts = jnp.pad(initial_model, ((0, 0), (0, padding), (0, 0)))
        parts = parts.reshape(layers, bands, own, cells).transpose(1, 0, 2, 3)
        data = jnp.pad(observed, ((0, padding), (0, 0)))
        data = data.reshape(bands, own, layers, cells // layers).transpose(0, 2, 1, 3)
        packed = jnp.concatenate([parts, data], -1)
    received = lax.all_to_all(packed.reshape(bands, held, width), "row", 0, 0, tiled=True)
    if not paired:
        received = received.reshape(bands, layers, own, width).transpose(1, 0, 2, 3)

    factors = [
        source_basis.transpose(0, 2, 1),
        receiver_basis.transpose(0, 2, 1),
        coupling.reshape(layers, bands * rank, rank),
    ]
    early = (layers, EARLY, cells, cells)
    *prepared, flipped_early = pl.pallas_call(
        ready_kernel,
        out_shape=[
            jax.ShapeDtypeStruct((layers, cells, LANES), bf16),
            jax.ShapeDtypeStruct((layers, cells, LANES), bf16),
            jax.ShapeDtypeStruct((layers, bands * rank, LANES), f32),
            jax.ShapeDtypeStruct((layers, bands * rank, LANES), f32),
            jax.ShapeDtypeStruct((LANES, cells), bf16),
            jax.ShapeDtypeStruct((layers, LANES, cells), bf16),
            pltpu.HBM(early, bf16),
        ],
        in_specs=[in_place()] * 4,
        out_specs=[whole_array()] * 6 + [in_place()],
        scratch_shapes=[pltpu.VMEM(value.shape, value.dtype) for value in factors]
        + [
            pltpu.VMEM(early, bf16),
            pltpu.VMEM(early, bf16),
            pltpu.SemaphoreType.DMA((3,)),
            pltpu.SemaphoreType.DMA((layers * EARLY,)),
            pltpu.SemaphoreType.DMA((layers * EARLY,)),
        ],
        compiler_params=pltpu.CompilerParams(vmem_limit_bytes=24 << 20),
        name="ready",
    )(*[stay(value) for value in factors], stay(near_tiles))
    limit = 4 * near_tiles.size + 40 * 4 * cols * cells
    result = pl.pallas_call(
        functools.partial(steps_kernel, bands=bands, own=own, rank=rank, paired=paired),
        out_shape=jax.ShapeDtypeStruct((rows, width), bf16),
        in_specs=[
            in_place(),
            whole_array(),
            in_place(),
            in_place(),
        ]
        + [whole_array()] * 6,
        out_specs=whole_array(),
        scratch_shapes=[
            pltpu.VMEM((layers, cols, cells), f32),
            pltpu.VMEM((cols, cells), f32),
            pltpu.VMEM((cols, cells), f32),
            pltpu.VMEM((layers, span, cols, cells), bf16),
            pltpu.VMEM((span, cols, cells), bf16),
            pltpu.VMEM(near_tiles.shape, bf16),
            pltpu.VMEM(near_tiles.shape, bf16),
            pltpu.SMEM((span,), jnp.int32),
            pltpu.SemaphoreType.DMA,
            pltpu.SemaphoreType.DMA((cells // STRIP, layers, span)),
            pltpu.SemaphoreType.DMA((layers, EARLY)),
        ],
        compiler_params=pltpu.CompilerParams(vmem_limit_bytes=limit),
        name="steps",
    )(
        stay(near_order),
        received.reshape(rows, width),
        stay(near_tiles),
        stay(flipped_early),
        *prepared,
    )
    if not paired:
        result = result.reshape(layers, bands, own, width).transpose(1, 0, 2, 3)
    returned = lax.all_to_all(result.reshape(bands, held, width), "row", 0, 0, tiled=True)
    if paired:
        return pl.pallas_call(
            functools.partial(unpack_kernel, own=own),
            out_shape=(
                jax.ShapeDtypeStruct((layers, perts, cells), f32),
                jax.ShapeDtypeStruct((perts, cells), f32),
            ),
            in_specs=[whole_array()],
            out_specs=(whole_array(), whole_array()),
            compiler_params=small,
            name="unpack",
        )(returned.reshape(rows, width))
    returned = returned.reshape(bands, layers, own, width).astype(f32)
    model = returned[..., :cells].transpose(1, 0, 2, 3).reshape(layers, cols, cells)
    misfit = returned[..., cells:].transpose(0, 2, 1, 3).reshape(cols, cells)
    return model[:, :perts], misfit[:perts]


def solution(mesh):
    placed = (P(), P(), P(), P(), P(), P(None, "group", "row"), P("group", "row"))
    return jax.shard_map(
        functools.partial(on_device, bands=mesh.shape["row"]),
        mesh=mesh,
        in_specs=placed,
        out_specs=(P(None, "group", "row"), P("group", "row")),
        check_vma=False,
    )
```

```python
import functools

import jax
import jax.numpy as jnp
from jax import lax
from jax.experimental import pallas as pl
from jax.experimental.pallas import tpu as pltpu
from jax.sharding import PartitionSpec as P

RADIUS = 2
ITERS = 3
SPAN = 2 * RADIUS + 1
STEP = 0.01
DAMPING = 10.0
COPIES = 3
LANES = 128
STRIP = 256
CHUNK = 512
SMALL = 8 << 20


def dot(left, right):
    return lax.dot_general(
        left, right, (((1,), (0,)), ((), ())), preferred_element_type=jnp.float32
    )


def dot_full(left, right):
    return lax.dot_general(
        left,
        right,
        (((1,), (0,)), ((), ())),
        precision=lax.Precision.HIGHEST,
        preferred_element_type=jnp.float32,
    )


def tables_kernel(
    source_ref,
    receiver_ref,
    ahead_ref,
    back_ref,
    source_wide,
    receiver_wide,
    core_ahead,
    core_back,
    receiver_rows,
    source_rows,
):
    layers, rank = source_ref.shape[:2]
    receiver_rows[...] = jnp.zeros_like(receiver_rows)
    source_rows[...] = jnp.zeros_like(source_rows)
    for l in range(layers):
        for c in range(COPIES):
            first = (l * COPIES + c) * rank
            receiver_rows[first : first + rank, :] = receiver_ref[l]
            source_rows[l, first : first + rank, :] = source_ref[l]
        source_wide[l] = jnp.concatenate([source_ref[l]] * (LANES // rank), 0).T
        receiver_wide[l] = jnp.concatenate([receiver_ref[l]] * (LANES // rank), 0).T
        before, after = l * COPIES * rank, LANES - (l + 1) * COPIES * rank
        for narrow, out in ((ahead_ref, core_ahead), (back_ref, core_back)):
            block = narrow[l]
            parts = [block] * COPIES
            if before:
                parts = [jnp.zeros((block.shape[0], before), jnp.float32)] + parts
            parts = parts + [jnp.zeros((block.shape[0], after), jnp.float32)]
            out[l] = jnp.concatenate(parts, 1)


def merged(first, second, own):
    lanes = first.shape[-1]
    first = first.reshape(-1, 2 * own, lanes)
    second = second.reshape(-1, 2 * own, lanes)
    low = lax.broadcasted_iota(jnp.int32, first.shape, 1) < own
    even = jnp.where(low, first, pltpu.roll(second, own, 1))
    odd = jnp.where(low, pltpu.roll(first, own, 1), second)
    return jnp.stack([even, odd], 1).reshape(-1, lanes)


def parted(values, own):
    pairs = values.reshape(-1, 2, 2 * own, values.shape[-1])
    low = lax.broadcasted_iota(jnp.int32, pairs[:, 0].shape, 1) < own
    even, odd = pairs[:, 0], pairs[:, 1]
    first = jnp.where(low, even, pltpu.roll(odd, own, 1))
    second = jnp.where(low, pltpu.roll(even, own, 1), odd)
    return first.reshape(-1, values.shape[-1]), second.reshape(-1, values.shape[-1])


def pack_kernel(model_hbm, data_hbm, out_ref, model_ref, data_ref, sems, *, own):
    cells = model_ref.shape[-1]
    half = cells // 2
    f32 = jnp.float32
    model_copy = pltpu.make_async_copy(model_hbm, model_ref, sems.at[0])
    data_copy = pltpu.make_async_copy(data_hbm, data_ref, sems.at[1])
    model_copy.start()
    data_copy.start()
    model_copy.wait()
    out_ref[:, :cells] = merged(
        model_ref[0].astype(f32), model_ref[1].astype(f32), own
    ).astype(out_ref.dtype)
    data_copy.wait()
    out_ref[:, cells:] = merged(
        data_ref[:, :half].astype(f32), data_ref[:, half:].astype(f32), own
    ).astype(out_ref.dtype)


def unpack_kernel(in_ref, model_ref, data_ref, *, own):
    cells = model_ref.shape[-1]
    half = cells // 2
    model_ref[0], model_ref[1] = parted(in_ref[:, :cells].astype(jnp.float32), own)
    data_ref[:, :half], data_ref[:, half:] = parted(
        in_ref[:, cells:].astype(jnp.float32), own
    )


def rolled(values, shift, own):
    shift = (shift * own) % values.shape[0]
    return pltpu.roll(values, shift, 0) if shift else values


def staircase(values, sign, rank, own):
    group = lax.broadcasted_iota(jnp.int32, values.shape, 1) // rank
    bit = 1
    while bit < LANES // rank:
        values = jnp.where((group & bit) != 0, rolled(values, sign * bit, own), values)
        bit *= 2
    return values


def split_parts(values, rank):
    part = (lax.broadcasted_iota(jnp.int32, values.shape, 1) // rank) % COPIES
    high = values.astype(jnp.bfloat16).astype(jnp.float32)
    rest = values - high
    middle = rest.astype(jnp.bfloat16).astype(jnp.float32)
    low = rest - middle
    return jnp.where(part == 0, high, jnp.where(part == 1, middle, low)).astype(jnp.bfloat16)


def steps_kernel(
    order_hbm,
    packed_in,
    tiles_hbm,
    source_wide,
    receiver_wide,
    core_ahead,
    core_back,
    receiver_rows,
    source_rows,
    packed_out,
    model,
    measured,
    misfit,
    wire,
    tiles,
    flipped,
    order_ref,
    order_sem,
    sems,
    *,
    bands,
    own,
    rank,
    paired,
):
    layers, span = tiles.shape[:2]
    cells = tiles.shape[3]
    share = cells // layers
    cols = bands * own

    def copy(j):
        part = pl.ds(j * STRIP, STRIP)
        return pltpu.make_async_copy(
            tiles_hbm.at[:, :, part, :], tiles.at[:, :, part, :], sems.at[j]
        )

    for j in range(cells // STRIP):
        copy(j).start()
    order = pltpu.make_async_copy(order_hbm, order_ref, order_sem)
    order.start()
    if paired:
        model[0], model[1] = parted(packed_in[:, :cells].astype(jnp.float32), own)
        measured[:, :share], measured[:, share:] = parted(
            packed_in[:, cells:].astype(jnp.float32), own
        )
    else:
        for l in range(layers):
            rows = slice(l * cols, (l + 1) * cols)
            model[l] = packed_in[rows, :cells].astype(jnp.float32)
            measured[:, l * share : (l + 1) * share] = packed_in[rows, cells:].astype(jnp.float32)

    order.wait()
    sent = wire.at[0]
    slots = []
    for offset in range(span):
        slot = jnp.int32(0)
        for k in range(1, span):
            slot = slot + jnp.where(order_ref[k] == offset, k, 0)
        slots.append(slot)
    groups = bands // (LANES // rank)

    def far(wide, cores, sign):
        total = jnp.zeros((cols, LANES), jnp.float32)
        for l in range(layers):
            stair = staircase(wide[l], sign, rank, own)

            def add(g, carry, l=l):
                moved, total = carry
                start = pl.multiple_of(g * LANES, LANES)
                total = total + dot_full(moved, cores[l, pl.ds(start, LANES), :])
                return rolled(moved, sign * (LANES // rank), own), total

            total = lax.fori_loop(0, groups, add, (stair, total), unroll=groups <= 2)[1]
        return split_parts(total, rank)

    def step(first):
        wide = []
        for l in range(layers):
            value = model[l]
            for offset in range(span):
                wire[l, slots[offset]] = rolled(value, offset - RADIUS, own).astype(jnp.bfloat16)
            wide.append(dot(value.astype(jnp.bfloat16), source_wide[l]))
        strips = cells // STRIP
        for j in range(strips):
            part = slice(j * STRIP, (j + 1) * STRIP)
            if first:
                copy(j).wait()
            predicted = None
            for l in range(layers):
                for k in range(span):
                    if first:
                        block = tiles[l, k, part, :].T
                        flipped[l, k, :, part] = block
                    else:
                        block = flipped[l, k, :, part]
                    term = dot(wire[l, k], block)
                    predicted = term if predicted is None else predicted + term
            misfit[:, part] = measured[:, part] - predicted
            if j == 0:
                field = far(wide, core_ahead, 1)
        residual = misfit[...] - dot(field, receiver_rows[...])
        misfit[...] = residual
        for offset in range(span):
            sent[slots[offset]] = rolled(residual, RADIUS - offset, own).astype(jnp.bfloat16)
        rounded = residual.astype(jnp.bfloat16)
        wide = [dot(rounded, receiver_wide[l]) for l in range(layers)]
        for l in range(layers):
            for j in range(cells // CHUNK):
                part = slice(j * CHUNK, (j + 1) * CHUNK)
                gradient = None
                for k in range(span):
                    term = dot(sent[k], tiles[l, k, :, part])
                    gradient = term if gradient is None else gradient + term
                if l + j == 0:
                    back = far(wide, core_back, -1)
                gradient = gradient + dot(back, source_rows[l, :, part])
                value = model[l, :, part]
                model[l, :, part] = value + STEP * (gradient - DAMPING * value)

    step(True)
    lax.fori_loop(1, ITERS, lambda index, carry: (step(False), carry)[1], 0)
    if paired:
        packed_out[:, :cells] = merged(model[0], model[1], own).astype(packed_out.dtype)
        packed_out[:, cells:] = merged(misfit[:, :share], misfit[:, share:], own).astype(
            packed_out.dtype
        )
    else:
        for l in range(layers):
            rows = slice(l * cols, (l + 1) * cols)
            packed_out[rows, :cells] = model[l].astype(packed_out.dtype)
            packed_out[rows, cells:] = misfit[:, l * share : (l + 1) * share].astype(
                packed_out.dtype
            )


def whole_array():
    return pl.BlockSpec(memory_space=pltpu.VMEM)


def in_place():
    return pl.BlockSpec(memory_space=pltpu.HBM)


def stay(value):
    return pltpu.with_memory_space_constraint(value, pltpu.HBM)


def on_device(
    near_tiles, near_order, receiver_basis, source_basis, coupling, initial_model, observed, *, bands
):
    layers, perts, cells = initial_model.shape
    rank = coupling.shape[-1]
    own = -(-perts // bands)
    held = layers * own
    rows = bands * held
    width = cells + cells // layers
    cols = bands * own
    bf16, f32 = jnp.bfloat16, jnp.float32

    paired = layers == 2 and layers * own == 8 and perts == cols
    small = pltpu.CompilerParams(vmem_limit_bytes=SMALL)
    if paired:
        packed = pl.pallas_call(
            functools.partial(pack_kernel, own=own),
            out_shape=jax.ShapeDtypeStruct((rows, width), bf16),
            in_specs=[in_place()] * 2,
            out_specs=whole_array(),
            scratch_shapes=[
                pltpu.VMEM(initial_model.shape, bf16),
                pltpu.VMEM(observed.shape, bf16),
                pltpu.SemaphoreType.DMA((2,)),
            ],
            compiler_params=small,
            name="pack",
        )(stay(initial_model), stay(observed))
    else:
        padding = cols - perts
        parts = jnp.pad(initial_model, ((0, 0), (0, padding), (0, 0)))
        parts = parts.reshape(layers, bands, own, cells).transpose(1, 0, 2, 3)
        data = jnp.pad(observed, ((0, padding), (0, 0)))
        data = data.reshape(bands, own, layers, cells // layers).transpose(0, 2, 1, 3)
        packed = jnp.concatenate([parts, data], -1)
    received = lax.all_to_all(packed.reshape(bands, held, width), "row", 0, 0, tiled=True)
    if not paired:
        received = received.reshape(bands, layers, own, width).transpose(1, 0, 2, 3)

    span = near_tiles.shape[1]
    tables = pl.pallas_call(
        tables_kernel,
        out_shape=[
            jax.ShapeDtypeStruct((layers, cells, LANES), bf16),
            jax.ShapeDtypeStruct((layers, cells, LANES), bf16),
            jax.ShapeDtypeStruct((layers, bands * rank, LANES), f32),
            jax.ShapeDtypeStruct((layers, bands * rank, LANES), f32),
            jax.ShapeDtypeStruct((LANES, cells), bf16),
            jax.ShapeDtypeStruct((layers, LANES, cells), bf16),
        ],
        in_specs=[whole_array()] * 4,
        out_specs=[whole_array()] * 6,
        compiler_params=small,
        name="tables",
    )(
        source_basis.transpose(0, 2, 1),
        receiver_basis.transpose(0, 2, 1),
        coupling.transpose(0, 1, 3, 2).reshape(layers, bands * rank, rank),
        coupling.reshape(layers, bands * rank, rank),
    )

    limit = 4 * near_tiles.size + 40 * 4 * cols * cells
    result = pl.pallas_call(
        functools.partial(steps_kernel, bands=bands, own=own, rank=rank, paired=paired),
        out_shape=jax.ShapeDtypeStruct((rows, width), bf16),
        in_specs=[
            in_place(),
            whole_array(),
            in_place(),
        ]
        + [whole_array()] * 6,
        out_specs=whole_array(),
        scratch_shapes=[
            pltpu.VMEM((layers, cols, cells), f32),
            pltpu.VMEM((cols, cells), f32),
            pltpu.VMEM((cols, cells), f32),
            pltpu.VMEM((layers, span, cols, cells), bf16),
            pltpu.VMEM(near_tiles.shape, bf16),
            pltpu.VMEM(near_tiles.shape, bf16),
            pltpu.SMEM((span,), jnp.int32),
            pltpu.SemaphoreType.DMA,
            pltpu.SemaphoreType.DMA((cells // STRIP,)),
        ],
        compiler_params=pltpu.CompilerParams(vmem_limit_bytes=limit),
        name="steps",
    )(
        stay(near_order),
        received.reshape(rows, width),
        stay(near_tiles),
        *tables,
    )
    if not paired:
        result = result.reshape(layers, bands, own, width).transpose(1, 0, 2, 3)
    returned = lax.all_to_all(result.reshape(bands, held, width), "row", 0, 0, tiled=True)
    if paired:
        return pl.pallas_call(
            functools.partial(unpack_kernel, own=own),
            out_shape=(
                jax.ShapeDtypeStruct((layers, perts, cells), f32),
                jax.ShapeDtypeStruct((perts, cells), f32),
            ),
            in_specs=[whole_array()],
            out_specs=(whole_array(), whole_array()),
            compiler_params=small,
            name="unpack",
        )(returned.reshape(rows, width))
    returned = returned.reshape(bands, layers, own, width).astype(f32)
    model = returned[..., :cells].transpose(1, 0, 2, 3).reshape(layers, cols, cells)
    misfit = returned[..., cells:].transpose(0, 2, 1, 3).reshape(cols, cells)
    return model[:, :perts], misfit[:perts]


def solution(mesh):
    placed = (P(), P(), P(), P(), P(), P(None, "group", "row"), P("group", "row"))
    return jax.shard_map(
        functools.partial(on_device, bands=mesh.shape["row"]),
        mesh=mesh,
        in_specs=placed,
        out_specs=(P(None, "group", "row"), P("group", "row")),
        check_vma=False,
    )
```

```python
import functools

import jax
import jax.numpy as jnp
from jax import lax
from jax.experimental import pallas as pl
from jax.experimental.pallas import tpu as pltpu
from jax.sharding import PartitionSpec as P

RADIUS = 2
ITERS = 3
SPAN = 2 * RADIUS + 1
STEP = 0.01
DAMPING = 10.0
COPIES = 3
LANES = 128
STRIP = 256
CHUNK = 512
SMALL = 8 << 20


def dot(left, right):
    return lax.dot_general(
        left, right, (((1,), (0,)), ((), ())), preferred_element_type=jnp.float32
    )


def dot_full(left, right):
    return lax.dot_general(
        left,
        right,
        (((1,), (0,)), ((), ())),
        precision=lax.Precision.HIGHEST,
        preferred_element_type=jnp.float32,
    )


def tables_kernel(
    source_ref,
    receiver_ref,
    ahead_ref,
    back_ref,
    source_wide,
    receiver_wide,
    core_ahead,
    core_back,
    receiver_rows,
    source_rows,
):
    layers, rank = source_ref.shape[:2]
    receiver_rows[...] = jnp.zeros_like(receiver_rows)
    source_rows[...] = jnp.zeros_like(source_rows)
    for l in range(layers):
        for c in range(COPIES):
            first = (l * COPIES + c) * rank
            receiver_rows[first : first + rank, :] = receiver_ref[l]
            source_rows[l, first : first + rank, :] = source_ref[l]
        source_wide[l] = jnp.concatenate([source_ref[l]] * (LANES // rank), 0).T
        receiver_wide[l] = jnp.concatenate([receiver_ref[l]] * (LANES // rank), 0).T
        before, after = l * COPIES * rank, LANES - (l + 1) * COPIES * rank
        for narrow, out in ((ahead_ref, core_ahead), (back_ref, core_back)):
            block = narrow[l]
            parts = [block] * COPIES
            if before:
                parts = [jnp.zeros((block.shape[0], before), jnp.float32)] + parts
            parts = parts + [jnp.zeros((block.shape[0], after), jnp.float32)]
            out[l] = jnp.concatenate(parts, 1)


def merged(first, second, own):
    lanes = first.shape[-1]
    first = first.reshape(-1, 2 * own, lanes)
    second = second.reshape(-1, 2 * own, lanes)
    low = lax.broadcasted_iota(jnp.int32, first.shape, 1) < own
    even = jnp.where(low, first, pltpu.roll(second, own, 1))
    odd = jnp.where(low, pltpu.roll(first, own, 1), second)
    return jnp.stack([even, odd], 1).reshape(-1, lanes)


def parted(values, own):
    pairs = values.reshape(-1, 2, 2 * own, values.shape[-1])
    low = lax.broadcasted_iota(jnp.int32, pairs[:, 0].shape, 1) < own
    even, odd = pairs[:, 0], pairs[:, 1]
    first = jnp.where(low, even, pltpu.roll(odd, own, 1))
    second = jnp.where(low, pltpu.roll(even, own, 1), odd)
    return first.reshape(-1, values.shape[-1]), second.reshape(-1, values.shape[-1])


def pack_kernel(model_hbm, data_hbm, out_ref, model_ref, data_ref, sems, *, own):
    cells = model_ref.shape[-1]
    half = cells // 2
    f32 = jnp.float32
    model_copy = pltpu.make_async_copy(model_hbm, model_ref, sems.at[0])
    data_copy = pltpu.make_async_copy(data_hbm, data_ref, sems.at[1])
    model_copy.start()
    data_copy.start()
    model_copy.wait()
    out_ref[:, :cells] = merged(
        model_ref[0].astype(f32), model_ref[1].astype(f32), own
    ).astype(out_ref.dtype)
    data_copy.wait()
    out_ref[:, cells:] = merged(
        data_ref[:, :half].astype(f32), data_ref[:, half:].astype(f32), own
    ).astype(out_ref.dtype)


def unpack_kernel(in_ref, model_ref, data_ref, *, own):
    cells = model_ref.shape[-1]
    half = cells // 2
    model_ref[0], model_ref[1] = parted(in_ref[:, :cells].astype(jnp.float32), own)
    data_ref[:, :half], data_ref[:, half:] = parted(
        in_ref[:, cells:].astype(jnp.float32), own
    )


def rolled(values, shift, own):
    shift = (shift * own) % values.shape[0]
    return pltpu.roll(values, shift, 0) if shift else values


def staircase(values, sign, rank, own):
    group = lax.broadcasted_iota(jnp.int32, values.shape, 1) // rank
    bit = 1
    while bit < LANES // rank:
        values = jnp.where((group & bit) != 0, rolled(values, sign * bit, own), values)
        bit *= 2
    return values


def split_parts(values, rank):
    part = (lax.broadcasted_iota(jnp.int32, values.shape, 1) // rank) % COPIES
    high = values.astype(jnp.bfloat16).astype(jnp.float32)
    rest = values - high
    middle = rest.astype(jnp.bfloat16).astype(jnp.float32)
    low = rest - middle
    return jnp.where(part == 0, high, jnp.where(part == 1, middle, low)).astype(jnp.bfloat16)


def steps_kernel(
    order_hbm,
    packed_in,
    tiles_hbm,
    source_wide,
    receiver_wide,
    core_ahead,
    core_back,
    receiver_rows,
    source_rows,
    packed_out,
    model,
    measured,
    misfit,
    wire,
    tiles,
    flipped,
    order_ref,
    order_sem,
    sems,
    *,
    bands,
    own,
    rank,
    paired,
):
    layers, span = tiles.shape[:2]
    cells = tiles.shape[3]
    share = cells // layers
    cols = bands * own

    def copy(j, l):
        part = pl.ds(j * STRIP, STRIP)
        return pltpu.make_async_copy(
            tiles_hbm.at[l, :, part, :], tiles.at[l, :, part, :], sems.at[j, l]
        )

    for j in range(cells // STRIP):
        for l in range(layers):
            copy(j, l).start()
    order = pltpu.make_async_copy(order_hbm, order_ref, order_sem)
    order.start()
    if paired:
        model[0], model[1] = parted(packed_in[:, :cells].astype(jnp.float32), own)
        measured[:, :share], measured[:, share:] = parted(
            packed_in[:, cells:].astype(jnp.float32), own
        )
    else:
        for l in range(layers):
            rows = slice(l * cols, (l + 1) * cols)
            model[l] = packed_in[rows, :cells].astype(jnp.float32)
            measured[:, l * share : (l + 1) * share] = packed_in[rows, cells:].astype(jnp.float32)

    order.wait()
    sent = wire.at[0]
    slots = []
    for offset in range(span):
        slot = jnp.int32(0)
        for k in range(1, span):
            slot = slot + jnp.where(order_ref[k] == offset, k, 0)
        slots.append(slot)
    groups = bands // (LANES // rank)

    def far(wide, cores, sign):
        total = jnp.zeros((cols, LANES), jnp.float32)
        for l in range(layers):
            stair = staircase(wide[l], sign, rank, own)

            def add(g, carry, l=l):
                moved, total = carry
                start = pl.multiple_of(g * LANES, LANES)
                total = total + dot_full(moved, cores[l, pl.ds(start, LANES), :])
                return rolled(moved, sign * (LANES // rank), own), total

            total = lax.fori_loop(0, groups, add, (stair, total), unroll=groups <= 2)[1]
        return split_parts(total, rank)

    def step(first):
        wide = []
        for l in range(layers):
            value = model[l]
            for offset in range(span):
                wire[l, slots[offset]] = rolled(value, offset - RADIUS, own).astype(jnp.bfloat16)
            wide.append(dot(value.astype(jnp.bfloat16), source_wide[l]))
        strips = cells // STRIP
        for j in range(strips):
            part = slice(j * STRIP, (j + 1) * STRIP)
            predicted = None
            for l in range(layers):
                if first:
                    copy(j, l).wait()
                for k in range(span):
                    if first:
                        block = tiles[l, k, part, :].T
                        flipped[l, k, :, part] = block
                    else:
                        block = flipped[l, k, :, part]
                    term = dot(wire[l, k], block)
                    predicted = term if predicted is None else predicted + term
            misfit[:, part] = measured[:, part] - predicted
            if j == 0:
                field = far(wide, core_ahead, 1)
        residual = misfit[...] - dot(field, receiver_rows[...])
        misfit[...] = residual
        for offset in range(span):
            sent[slots[offset]] = rolled(residual, RADIUS - offset, own).astype(jnp.bfloat16)
        rounded = residual.astype(jnp.bfloat16)
        wide = [dot(rounded, receiver_wide[l]) for l in range(layers)]
        for l in range(layers):
            for j in range(cells // CHUNK):
                part = slice(j * CHUNK, (j + 1) * CHUNK)
                gradient = None
                for k in range(span):
                    term = dot(sent[k], tiles[l, k, :, part])
                    gradient = term if gradient is None else gradient + term
                if l + j == 0:
                    back = far(wide, core_back, -1)
                gradient = gradient + dot(back, source_rows[l, :, part])
                value = model[l, :, part]
                model[l, :, part] = value + STEP * (gradient - DAMPING * value)

    step(True)
    lax.fori_loop(1, ITERS, lambda index, carry: (step(False), carry)[1], 0)
    if paired:
        packed_out[:, :cells] = merged(model[0], model[1], own).astype(packed_out.dtype)
        packed_out[:, cells:] = merged(misfit[:, :share], misfit[:, share:], own).astype(
            packed_out.dtype
        )
    else:
        for l in range(layers):
            rows = slice(l * cols, (l + 1) * cols)
            packed_out[rows, :cells] = model[l].astype(packed_out.dtype)
            packed_out[rows, cells:] = misfit[:, l * share : (l + 1) * share].astype(
                packed_out.dtype
            )


def whole_array():
    return pl.BlockSpec(memory_space=pltpu.VMEM)


def in_place():
    return pl.BlockSpec(memory_space=pltpu.HBM)


def stay(value):
    return pltpu.with_memory_space_constraint(value, pltpu.HBM)


def on_device(
    near_tiles, near_order, receiver_basis, source_basis, coupling, initial_model, observed, *, bands
):
    layers, perts, cells = initial_model.shape
    rank = coupling.shape[-1]
    own = -(-perts // bands)
    held = layers * own
    rows = bands * held
    width = cells + cells // layers
    cols = bands * own
    bf16, f32 = jnp.bfloat16, jnp.float32

    paired = layers == 2 and layers * own == 8 and perts == cols
    small = pltpu.CompilerParams(vmem_limit_bytes=SMALL)
    if paired:
        packed = pl.pallas_call(
            functools.partial(pack_kernel, own=own),
            out_shape=jax.ShapeDtypeStruct((rows, width), bf16),
            in_specs=[in_place()] * 2,
            out_specs=whole_array(),
            scratch_shapes=[
                pltpu.VMEM(initial_model.shape, bf16),
                pltpu.VMEM(observed.shape, bf16),
                pltpu.SemaphoreType.DMA((2,)),
            ],
            compiler_params=small,
            name="pack",
        )(stay(initial_model), stay(observed))
    else:
        padding = cols - perts
        parts = jnp.pad(initial_model, ((0, 0), (0, padding), (0, 0)))
        parts = parts.reshape(layers, bands, own, cells).transpose(1, 0, 2, 3)
        data = jnp.pad(observed, ((0, padding), (0, 0)))
        data = data.reshape(bands, own, layers, cells // layers).transpose(0, 2, 1, 3)
        packed = jnp.concatenate([parts, data], -1)
    received = lax.all_to_all(packed.reshape(bands, held, width), "row", 0, 0, tiled=True)
    if not paired:
        received = received.reshape(bands, layers, own, width).transpose(1, 0, 2, 3)

    span = near_tiles.shape[1]
    tables = pl.pallas_call(
        tables_kernel,
        out_shape=[
            jax.ShapeDtypeStruct((layers, cells, LANES), bf16),
            jax.ShapeDtypeStruct((layers, cells, LANES), bf16),
            jax.ShapeDtypeStruct((layers, bands * rank, LANES), f32),
            jax.ShapeDtypeStruct((layers, bands * rank, LANES), f32),
            jax.ShapeDtypeStruct((LANES, cells), bf16),
            jax.ShapeDtypeStruct((layers, LANES, cells), bf16),
        ],
        in_specs=[whole_array()] * 4,
        out_specs=[whole_array()] * 6,
        compiler_params=small,
        name="tables",
    )(
        source_basis.transpose(0, 2, 1),
        receiver_basis.transpose(0, 2, 1),
        coupling.transpose(0, 1, 3, 2).reshape(layers, bands * rank, rank),
        coupling.reshape(layers, bands * rank, rank),
    )

    limit = 4 * near_tiles.size + 40 * 4 * cols * cells
    result = pl.pallas_call(
        functools.partial(steps_kernel, bands=bands, own=own, rank=rank, paired=paired),
        out_shape=jax.ShapeDtypeStruct((rows, width), bf16),
        in_specs=[
            in_place(),
            whole_array(),
            in_place(),
        ]
        + [whole_array()] * 6,
        out_specs=whole_array(),
        scratch_shapes=[
            pltpu.VMEM((layers, cols, cells), f32),
            pltpu.VMEM((cols, cells), f32),
            pltpu.VMEM((cols, cells), f32),
            pltpu.VMEM((layers, span, cols, cells), bf16),
            pltpu.VMEM(near_tiles.shape, bf16),
            pltpu.VMEM(near_tiles.shape, bf16),
            pltpu.SMEM((span,), jnp.int32),
            pltpu.SemaphoreType.DMA,
            pltpu.SemaphoreType.DMA((cells // STRIP, layers)),
        ],
        compiler_params=pltpu.CompilerParams(vmem_limit_bytes=limit),
        name="steps",
    )(
        stay(near_order),
        received.reshape(rows, width),
        stay(near_tiles),
        *tables,
    )
    if not paired:
        result = result.reshape(layers, bands, own, width).transpose(1, 0, 2, 3)
    returned = lax.all_to_all(result.reshape(bands, held, width), "row", 0, 0, tiled=True)
    if paired:
        return pl.pallas_call(
            functools.partial(unpack_kernel, own=own),
            out_shape=(
                jax.ShapeDtypeStruct((layers, perts, cells), f32),
                jax.ShapeDtypeStruct((perts, cells), f32),
            ),
            in_specs=[whole_array()],
            out_specs=(whole_array(), whole_array()),
            compiler_params=small,
            name="unpack",
        )(returned.reshape(rows, width))
    returned = returned.reshape(bands, layers, own, width).astype(f32)
    model = returned[..., :cells].transpose(1, 0, 2, 3).reshape(layers, cols, cells)
    misfit = returned[..., cells:].transpose(0, 2, 1, 3).reshape(cols, cells)
    return model[:, :perts], misfit[:perts]


def solution(mesh):
    placed = (P(), P(), P(), P(), P(), P(None, "group", "row"), P("group", "row"))
    return jax.shard_map(
        functools.partial(on_device, bands=mesh.shape["row"]),
        mesh=mesh,
        in_specs=placed,
        out_specs=(P(None, "group", "row"), P("group", "row")),
        check_vma=False,
    )
```
